256 devices in a mesh: occ: 32 (over z, x_hi, core), vir: 8 (over x_lo, y).
Axes of the slice: x: 4 (x_hi: 2, x_lo: 2; x = x_hi * 2 + x_lo), y: 4, z: 8, core: 2. Of those that a mesh axis runs over, the one named last changes fastest.
Arguments:
- factors: bfloat16 [32, 1024, 3072], P('occ', 'vir'), may hold values from -0.71875 to 0.71875
- occ_energy: float32 [32], replicated, may hold values from -2 to -0.4
- vir_energy: float32 [1024], replicated, may hold values from 0.4 to 4
- density_in: float32 [32, 1024, 3072], P('occ', 'vir'), may hold values from -3 to 3
Outputs:
- density: float32 [32, 1024, 3072], P('occ', 'vir')
The draws below stay inside these ranges and needn't reach their ends.
All inputs are finite; a program needn't handle non-finite values.
Results may differ from the reference program's by a relative error of at most 0.0027.
Values may be sent and summed in bfloat16 or wider, within the bound.
No kernel may reach another device: no remote copies, remote signals or barrier semaphores. Data moves between devices by JAX's collectives and lax.ppermute only.
A program may use at most 128 MiB of HBM per device.

```python
import jax
import jax.numpy as jnp
from jax import lax

V = 1024
X = 3072
OCC_DEV = 1
VISITS = 3
OCC = 32
N_OCC = 32


def block_scale(key, extent, cuts, low, largest):
    gain, own = 1.0, jax.random.fold_in(key, 6)
    for axis_at, parts in cuts:
        steps = jnp.exp(jax.random.uniform(jax.random.fold_in(own, axis_at), (parts,), jnp.float32, low / len(cuts), largest / len(cuts)))
        gain = gain * jnp.repeat(steps, extent[axis_at] // parts).reshape([-1 if axis == axis_at else 1 for axis in range(len(extent))])
    return gain


def gaussian(stream_key, shape, deviation, most, shards=(), held_as=jnp.bfloat16):
    drawn = deviation * jax.random.normal(stream_key, shape, jnp.float32)
    if shards:
        drawn = drawn * block_scale(stream_key, shape, shards, -0.22, 0.18)
    return jnp.clip(drawn, -most, most).astype(held_as)


def setup_inputs(seed: int = 0) -> dict:
    arg_keys = jax.random.split(jax.random.key(seed), 5)
    return {
        "factors": gaussian(arg_keys[0], (OCC, V, X), 0.12, 0.71875, ((0, 32), (1, 8))),
        "occ_energy": jnp.clip(jax.random.uniform(arg_keys[1], (OCC,), jnp.float32, -2.0, -0.4), -2.0, -0.4),
        "vir_energy": jnp.clip(jax.random.uniform(arg_keys[2], (V,), jnp.float32, 0.4, 4.0), 0.4, 4.0),
        "density_in": gaussian(arg_keys[3], (OCC, V, X), 0.5, 3.0, ((0, 32), (1, 8)), jnp.float32),
    }


def to_half(value):
    return lax.optimization_barrier(value.astype(jnp.bfloat16)).astype(jnp.float32)


def reference(factors, occ_energy, vir_energy, density_in):
    widened = factors.astype(jnp.float32)

    def one_block(block):
        start = (block * OCC_DEV).astype(jnp.int32)
        own = lax.dynamic_slice_in_dim(widened, start, OCC_DEV, 0)
        e_own = lax.dynamic_slice_in_dim(occ_energy, start, OCC_DEV, 0)
        total = jnp.zeros((OCC_DEV * V, X), jnp.float32)
        for visit in range(VISITS):
            other = (((block - visit) % N_OCC) * OCC_DEV).astype(jnp.int32)
            partner = lax.dynamic_slice_in_dim(widened, other, OCC_DEV, 0)
            e_partner = lax.dynamic_slice_in_dim(occ_energy, other, OCC_DEV, 0)
            direct = jnp.dot(own.reshape(OCC_DEV * V, X), partner.reshape(OCC_DEV * V, X).T,
                             precision=lax.Precision.HIGHEST)
            tile = to_half(direct).reshape(OCC_DEV, V, OCC_DEV, V)
            swapped = tile.transpose(0, 3, 2, 1)
            denom = (e_own[:, None, None, None] + e_partner[None, None, :, None]
                     - vir_energy[None, :, None, None] - vir_energy[None, None, None, :])
            amp = to_half((2.0 * tile - swapped) / denom)
            total = total + jnp.dot(amp.reshape(OCC_DEV * V, OCC_DEV * V), partner.reshape(OCC_DEV * V, X),
                                    precision=lax.Precision.HIGHEST)
        return total.reshape(OCC_DEV, V, X)

    blocks = lax.map(one_block, jnp.arange(N_OCC, dtype=jnp.int32))
    return density_in + blocks.reshape(OCC_DEV * N_OCC, V, X)
```

```python
import functools

import jax
import jax.numpy as jnp
from jax import lax
from jax.experimental import pallas as pl
from jax.experimental.pallas import tpu as pltpu
from jax.sharding import Mesh
from jax.sharding import PartitionSpec as P

Z, XH, CORE, XL, Y = 8, 2, 2, 2, 4
GROUPS = Z * XH
AXES = ("z", "xh", "core", "xl", "y")
PLACE = ("z", "xh", "core", "xl")
SLAB = 128
N_SLABS = CORE * Y
STEP = 512
BF16, F32 = jnp.bfloat16, jnp.float32


def place(group, core, xl):
    return ((group % GROUPS) * CORE + core) * XL + xl


def homes_of_workers(shift):
    pairs = []
    for g in range(GROUPS):
        for c in range(CORE):
            for r in range(XL):
                i = 2 * g + r + shift
                pairs.append((place(i // 2, i % 2, c), place(g, c, r)))
    return pairs


def to_workers(block, shift):
    return lax.ppermute(block, PLACE, homes_of_workers(shift))


def to_homes(block, shift):
    return lax.ppermute(block, PLACE, [(w, h) for h, w in homes_of_workers(shift)])


def along_y(block, step):
    pairs = []
    for c in range(CORE):
        sign = 1 - 2 * c
        for y in range(Y):
            pairs.append((c * Y + y, c * Y + (y + sign * step) % Y))
    return lax.ppermute(block, ("core", "y"), pairs)


def to_sibling(block):
    return lax.ppermute(block, "core", [(0, 1), (1, 0)])


def slab_of(q):
    core, y = lax.axis_index("core"), lax.axis_index("y")
    kind, sibling = q // 2, q % 2
    core = 1 - core if sibling else core
    sign = 1 - 2 * core
    y = lax.rem(y + sign * (0, -1, 1, 2)[kind] + 2 * Y, Y)
    return core * Y + y


def integrals_kernel(*refs):
    rows, pieces = refs[:3], refs[3 : 3 + N_SLABS]
    direct_ref, sent_ref, total = refs[3 + N_SLABS :]
    k = pl.program_id(0)
    left = jnp.concatenate([r[...] for r in rows], axis=0)
    right = jnp.concatenate([r[...] for r in pieces], axis=0)
    part = lax.dot_general(left, right, (((1,), (1,)), ((), ())), preferred_element_type=F32)

    @pl.when(k == 0)
    def _():
        total[...] = part

    @pl.when(k > 0)
    def _():
        total[...] += part

    @pl.when(k == pl.num_programs(0) - 1)
    def _():
        direct_ref[...] = total[...].astype(BF16)
        for q in range(N_SLABS):
            for v in range(2):
                tile = total[(v + 1) * SLAB : (v + 2) * SLAB, q * SLAB : (q + 1) * SLAB]
                sent_ref[slab_of(q), v] = tile.T.astype(BF16)


def integrals(rows, pieces):
    width = rows[0].shape[1]
    spec = pl.BlockSpec((SLAB, STEP), lambda k: (0, k))
    return pl.pallas_call(
        integrals_kernel,
        grid=(width // STEP,),
        in_specs=[spec] * (3 + N_SLABS),
        out_specs=[
            pl.BlockSpec((3 * SLAB, N_SLABS * SLAB), lambda k: (0, 0)),
            pl.BlockSpec((N_SLABS, 2, SLAB, SLAB), lambda k: (0, 0, 0, 0)),
        ],
        out_shape=[
            jax.ShapeDtypeStruct((3 * SLAB, N_SLABS * SLAB), BF16),
            jax.ShapeDtypeStruct((N_SLABS, 2, SLAB, SLAB), BF16),
        ],
        scratch_shapes=[pltpu.VMEM((3 * SLAB, N_SLABS * SLAB), F32)],
        cost_estimate=pl.CostEstimate(
            flops=2 * 3 * SLAB * N_SLABS * SLAB * width,
            bytes_accessed=(3 + N_SLABS) * SLAB * width * 2,
            transcendentals=0,
        ),
        compiler_params=pltpu.CompilerParams(vmem_limit_bytes=40 << 20),
        name="integrals",
    )(*rows, *pieces)


def density_kernel(visits, has_swapped, *refs):
    e_occ, e_vir, direct_ref = refs[:3]
    at = 3
    if has_swapped:
        swapped_ref = refs[at]
        at += 1
    pieces, refs = refs[at : at + N_SLABS], refs[at + N_SLABS :]
    outs, amp = refs[: len(visits)], refs[len(visits)]
    k = pl.program_id(0)

    @pl.when(k == 0)
    def _():
        group = lax.axis_index("z") * XH + lax.axis_index("xh")
        j = 2 * group + lax.axis_index("xl")
        own = slab_of(0)
        e_a = jnp.broadcast_to(e_vir[own], (SLAB, SLAB)).T
        for n, v in enumerate(visits):
            pair = e_occ[lax.rem(j + v, 2 * GROUPS)] + e_occ[j]
            for q in range(N_SLABS):
                slab = slab_of(q)
                d = direct_ref[v * SLAB : (v + 1) * SLAB, q * SLAB : (q + 1) * SLAB].astype(F32)
                s = d if v == 0 else swapped_ref[slab, v - 1].astype(F32)
                denom = pair - e_a - e_vir[slab]
                amp[n * SLAB : (n + 1) * SLAB, q * SLAB : (q + 1) * SLAB] = ((2.0 * d - s) / denom).astype(BF16)

    right = jnp.concatenate([r[...] for r in pieces], axis=0)
    out = jnp.dot(amp[...], right, preferred_element_type=F32)
    for n in range(len(visits)):
        outs[n][...] = out[n * SLAB : (n + 1) * SLAB].astype(BF16)


def density(visits, e_occ, e_vir, direct, swapped, pieces):
    width = pieces[0].shape[1]
    spec = pl.BlockSpec((SLAB, STEP), lambda k: (0, k))
    whole = lambda *shape: pl.BlockSpec(shape, lambda k: (0,) * len(shape))
    has_swapped = swapped is not None
    rows = len(visits) * SLAB
    return pl.pallas_call(
        functools.partial(density_kernel, visits, has_swapped),
        grid=(width // STEP,),
        in_specs=[pl.BlockSpec(memory_space=pltpu.SMEM), whole(N_SLABS, 1, SLAB), whole(3 * SLAB, N_SLABS * SLAB)]
        + ([whole(N_SLABS, 2, SLAB, SLAB)] if has_swapped else [])
        + [spec] * N_SLABS,
        out_specs=[spec] * len(visits),
        out_shape=[jax.ShapeDtypeStruct((SLAB, width), BF16)] * len(visits),
        scratch_shapes=[pltpu.VMEM((rows, N_SLABS * SLAB), BF16)],
        cost_estimate=pl.CostEstimate(
            flops=2 * rows * N_SLABS * SLAB * width,
            bytes_accessed=(len(visits) + N_SLABS) * SLAB * width * 2,
            transcendentals=0,
        ),
        compiler_params=pltpu.CompilerParams(vmem_limit_bytes=40 << 20),
        name="density",
    )(e_occ, e_vir, direct, *([swapped] if has_swapped else []), *pieces)


def on_device(factors, occ_energy, vir_energy, density_in):
    width = factors.shape[2]
    home = factors.reshape(SLAB, width)
    own = to_workers(home, 0)
    next_1 = to_workers(home, 1)
    next_2 = to_workers(home, 2)
    one = along_y(own, 1)
    other = along_y(own, -1)
    two = along_y(one, 1)
    mine = [own, one, other, two]
    pieces = []
    for piece in mine:
        pieces += [piece, to_sibling(piece)]
    e_vir = vir_energy.reshape(N_SLABS, 1, SLAB)
    direct, sent = integrals([own, next_1, next_2], pieces)
    swapped = lax.all_to_all(sent, ("core", "y"), split_axis=0, concat_axis=0, tiled=True)
    (part_0,) = density((0,), occ_energy, e_vir, direct, None, pieces)
    part_1, part_2 = density((1, 2), occ_energy, e_vir, direct, swapped, pieces)
    total = density_in.reshape(SLAB, width)
    for shift, part in enumerate((part_0, part_1, part_2)):
        total = total + to_homes(part, shift).astype(F32)
    return total.reshape(density_in.shape)


def solution(mesh):
    fine = Mesh(mesh.devices.reshape(Z, XH, CORE, XL, Y), AXES)
    split = P(("z", "xh", "core"), ("xl", "y"), None)
    return jax.shard_map(
        on_device,
        mesh=fine,
        in_specs=(split, P(), P(), split),
        out_specs=split,
        check_vma=False,
    )
```

```python
import functools

import jax
import jax.numpy as jnp
from jax import lax
from jax.experimental import pallas as pl
from jax.experimental.pallas import tpu as pltpu
from jax.sharding import Mesh
from jax.sharding import PartitionSpec as P

Z, XH, CORE, XL, Y = 8, 2, 2, 2, 4
GROUPS = Z * XH
AXES = ("z", "xh", "core", "xl", "y")
PLACE = ("z", "xh", "core", "xl")
SLAB = 128
N_SLABS = CORE * Y
STEP = 512
EARLY = 6
BF16, F32 = jnp.bfloat16, jnp.float32


def place(group, core, xl):
    return ((group % GROUPS) * CORE + core) * XL + xl


def homes_of_workers(shift):
    pairs = []
    for g in range(GROUPS):
        for c in range(CORE):
            for r in range(XL):
                i = 2 * g + r + shift
                pairs.append((place(i // 2, i % 2, c), place(g, c, r)))
    return pairs


def to_workers(block, shift):
    return lax.ppermute(block, PLACE, homes_of_workers(shift))


def to_homes(block, shift):
    return lax.ppermute(block, PLACE, [(w, h) for h, w in homes_of_workers(shift)])


def along_y(block, step):
    pairs = []
    for c in range(CORE):
        sign = 1 - 2 * c
        for y in range(Y):
            pairs.append((c * Y + y, c * Y + (y + sign * step) % Y))
    return lax.ppermute(block, ("core", "y"), pairs)


def to_sibling(block):
    return lax.ppermute(block, "core", [(0, 1), (1, 0)])


def exchanged(tiles):
    def across(block, step):
        pairs = []
        for c in range(CORE):
            sign = 1 - 2 * c
            for y in range(Y):
                pairs.append((c * Y + y, (1 - c) * Y + (y + sign * step) % Y))
        return lax.ppermute(block, ("core", "y"), pairs)

    beside, down, beside_down, up, beside_up, far, beside_far = tiles
    return [
        to_sibling(beside),
        along_y(up, 1),
        across(beside_down, 1),
        along_y(down, -1),
        across(beside_up, -1),
        along_y(far, 2),
        across(beside_far, 2),
    ]


def slab_of(q):
    core, y = lax.axis_index("core"), lax.axis_index("y")
    kind, sibling = q // 2, q % 2
    core = 1 - core if sibling else core
    sign = 1 - 2 * core
    y = lax.rem(y + sign * (0, -1, 1, 2)[kind] + 2 * Y, Y)
    return core * Y + y


def integrals_kernel(count, *refs):
    rows, pieces, refs = refs[:3], refs[3 : 3 + count], refs[3 + count :]
    direct_ref, tile_refs, total = refs[0], refs[1:-1], refs[-1]
    total[...] = jnp.zeros_like(total)

    @pl.loop(0, rows[0].shape[1] // STEP)
    def _(k):
        part = pl.ds(pl.multiple_of(k * STEP, STEP), STEP)
        left = jnp.concatenate([r[:, part] for r in rows], axis=0)
        right = jnp.concatenate([r[:, part] for r in pieces], axis=0)
        total[...] += lax.dot_general(left, right, (((1,), (1,)), ((), ())), preferred_element_type=F32)

    direct_ref[...] = total[...].astype(BF16)
    for at, tile_ref in enumerate(tile_refs, start=count - len(tile_refs)):
        for v in range(2):
            tile_ref[v] = total[(v + 1) * SLAB : (v + 2) * SLAB, at * SLAB : (at + 1) * SLAB].T.astype(BF16)


def in_vmem(count):
    return [pl.BlockSpec(memory_space=pltpu.VMEM)] * count


def integrals(rows, pieces, tiles):
    width = rows[0].shape[1]
    count = len(pieces)
    columns = count * SLAB
    return pl.pallas_call(
        functools.partial(integrals_kernel, count),
        in_specs=in_vmem(3 + count),
        out_specs=in_vmem(1 + tiles),
        out_shape=[jax.ShapeDtypeStruct((3 * SLAB, columns), BF16)]
        + [jax.ShapeDtypeStruct((2, SLAB, SLAB), BF16)] * tiles,
        scratch_shapes=[pltpu.VMEM((3 * SLAB, columns), F32)],
        cost_estimate=pl.CostEstimate(
            flops=2 * 3 * SLAB * columns * width,
            bytes_accessed=(3 + count) * SLAB * width * 2,
            transcendentals=0,
        ),
        compiler_params=pltpu.CompilerParams(vmem_limit_bytes=12 << 20),
        name="integrals",
    )(*rows, *pieces)


def density_kernel(visits, has_swapped, *refs):
    (e_occ, e_vir, early_ref, late_ref), refs = refs[:4], refs[4:]
    if has_swapped:
        swapped_refs, refs = (None, *refs[: N_SLABS - 1]), refs[N_SLABS - 1 :]
    pieces, refs = refs[:N_SLABS], refs[N_SLABS:]
    outs, amp = refs[: len(visits)], refs[len(visits)]
    group = lax.axis_index("z") * XH + lax.axis_index("xh")
    j = 2 * group + lax.axis_index("xl")
    e_a = jnp.broadcast_to(e_vir[slab_of(0)], (SLAB, SLAB)).T
    for n, v in enumerate(visits):
        pair = e_occ[lax.rem(j + v, 2 * GROUPS)] + e_occ[j]
        for q in range(N_SLABS):
            slab = slab_of(q)
            direct_ref, p = (early_ref, q) if q < EARLY else (late_ref, q - EARLY)
            d = direct_ref[v * SLAB : (v + 1) * SLAB, p * SLAB : (p + 1) * SLAB].astype(F32)
            if v == 0:
                s = d
            elif q == 0:
                s = d.T
            else:
                s = swapped_refs[q][v - 1].astype(F32)
            denom = pair - e_a - e_vir[slab]
            amp[n * SLAB : (n + 1) * SLAB, q * SLAB : (q + 1) * SLAB] = ((2.0 * d - s) / denom).astype(BF16)

    @pl.loop(0, pieces[0].shape[1] // STEP)
    def _(k):
        part = pl.ds(pl.multiple_of(k * STEP, STEP), STEP)
        right = jnp.concatenate([r[:, part] for r in pieces], axis=0)
        out = jnp.dot(amp[...], right, preferred_element_type=F32)
        for n in range(len(visits)):
            outs[n][:, part] = out[n * SLAB : (n + 1) * SLAB].astype(BF16)


def density(visits, e_occ, e_vir, direct, swapped, pieces):
    width = pieces[0].shape[1]
    rows = len(visits) * SLAB
    operands = [e_vir, *direct] + ([] if swapped is None else swapped) + pieces
    return pl.pallas_call(
        functools.partial(density_kernel, visits, swapped is not None),
        in_specs=[pl.BlockSpec(memory_space=pltpu.SMEM)] + in_vmem(len(operands)),
        out_specs=in_vmem(len(visits)),
        out_shape=[jax.ShapeDtypeStruct((SLAB, width), BF16)] * len(visits),
        scratch_shapes=[pltpu.VMEM((rows, N_SLABS * SLAB), BF16)],
        cost_estimate=pl.CostEstimate(
            flops=2 * rows * N_SLABS * SLAB * width,
            bytes_accessed=(len(visits) + N_SLABS) * SLAB * width * 2,
            transcendentals=0,
        ),
        compiler_params=pltpu.CompilerParams(vmem_limit_bytes=12 << 20),
        name="density",
    )(e_occ, *operands)


def on_device(factors, occ_energy, vir_energy, density_in):
    width = factors.shape[2]
    home = factors.reshape(SLAB, width)
    own = (to_workers(home, 0))
    next_1 = (to_workers(home, 1))
    next_2 = (to_workers(home, 2))
    one = (along_y(own, 1))
    other = (along_y(own, -1))
    two = (along_y(one, 1))
    mine = [own, one, other, two]
    pieces = []
    for piece in mine:
        pieces += [piece, (to_sibling(piece))]
    e_vir = vir_energy.reshape(N_SLABS, 1, SLAB)
    rows = [own, next_1, next_2]
    early, *tiles = integrals(rows, pieces[:EARLY], EARLY - 1)
    late, *last_tiles = integrals(rows, pieces[EARLY:], N_SLABS - EARLY)
    direct = (early, late)
    swapped = exchanged(tiles + last_tiles)
    (part_0,) = density((0,), occ_energy, e_vir, direct, None, pieces)
    part_1, part_2 = density((1, 2), occ_energy, e_vir, direct, swapped, pieces)
    total = density_in.reshape(SLAB, width)
    for shift, part in enumerate((part_0, part_1, part_2)):
        total = total + to_homes(part, shift).astype(F32)
    return total.reshape(density_in.shape)


def solution(mesh):
    fine = Mesh(mesh.devices.reshape(Z, XH, CORE, XL, Y), AXES)
    split = P(("z", "xh", "core"), ("xl", "y"), None)
    return jax.shard_map(
        on_device,
        mesh=fine,
        in_specs=(split, P(), P(), split),
        out_specs=split,
        check_vma=False,
    )
```

```python
import functools

import jax
import jax.numpy as jnp
from jax import lax
from jax.experimental import pallas as pl
from jax.experimental.pallas import tpu as pltpu
from jax.sharding import Mesh
from jax.sharding import PartitionSpec as P

Z, XH, CORE, XL, Y = 8, 2, 2, 2, 4
GROUPS = Z * XH
AXES = ("z", "xh", "core", "xl", "y")
SLAB = 128
N_SLABS = XL * Y
PIECES = ((0, 0), (0, -1), (0, 1), (0, 2), (1, 0), (1, -1), (1, 1), (1, 2))
BACK = (0, 2, 1, 3, 4, 6, 5, 7)
STEP = 512
EARLY = 7
TURNED = 4
BF16, F32 = jnp.bfloat16, jnp.float32


def two_blocks_on(block, step):
    pairs = []
    for g in range(GROUPS):
        for c in range(CORE):
            for x in range(XL):
                to = (g + step) % GROUPS * CORE + c
                pairs.append(((g * CORE + c) * XL + x, to * XL + 1 - x))
    return lax.ppermute(block, ("z", "xh", "core", "xl"), pairs)


def one_block_on(block, core):
    return lax.ppermute(block, ("core", "xl"), [(core * XL + x, (1 - core) * XL + (x if core else 1 - x)) for x in range(XL)])


def to_sibling(block):
    return lax.ppermute(block, "core", [(0, 1), (1, 0)])


def within(block, across, step):
    pairs = []
    for c in range(CORE):
        sign = 1 - 2 * c
        for x in range(XL):
            for y in range(Y):
                to = (x ^ across) * Y + (y + sign * step) % Y
                pairs.append((c * N_SLABS + x * Y + y, c * N_SLABS + to))
    return lax.ppermute(block, ("core", "xl", "y"), pairs)


def after(block, *done):
    return lax.optimization_barrier((block, *done))[0]


def gathered(home):
    cross = within(home, 1, 0)
    down = within(home, 0, 1)
    up = within(home, 0, -1)
    far = within(down, 0, 1)
    cross_up = within(up, 1, 0)
    cross_down = within(after(cross, down, up), 0, 1)
    cross_far = within(after(cross_down, far), 0, 1)
    return [home, down, up, far, cross, cross_down, cross_up, cross_far]


def exchanged(tiles):
    return {BACK[q]: within(tile, 1 - PIECES[q][0], PIECES[q][1]) for q, tile in tiles.items()}


def slab_of(q):
    across, step = PIECES[q]
    x, y = lax.axis_index("xl"), lax.axis_index("y")
    x = 1 - x if across else x
    return x * Y + lax.rem(y + step * (1 - 2 * lax.axis_index("core")) + Y, Y)


def in_vmem(count):
    return [pl.BlockSpec(memory_space=pltpu.VMEM)] * count


def integrals_kernel(count, sent, *refs):
    rows, pieces, refs = refs[:3], refs[3 : 3 + count], refs[3 + count :]
    direct_ref, tile_refs, total = refs[0], refs[1:-1], refs[-1]
    total[...] = jnp.zeros_like(total)

    @pl.loop(0, rows[0].shape[1] // STEP)
    def _(k):
        part = pl.ds(pl.multiple_of(k * STEP, STEP), STEP)
        left = jnp.concatenate([r[:, part] for r in rows], axis=0)
        right = jnp.concatenate([r[:, part] for r in pieces], axis=0)
        total[...] += lax.dot_general(left, right, (((1,), (1,)), ((), ())), preferred_element_type=F32)

    direct_ref[...] = total[...].astype(BF16)
    for at, tile_ref in zip(sent, tile_refs):
        for v in range(2):
            tile_ref[v] = total[(v + 1) * SLAB : (v + 2) * SLAB, at * SLAB : (at + 1) * SLAB].T.astype(BF16)


def integrals(rows, pieces, sent):
    width = rows[0].shape[1]
    count = len(pieces)
    columns = count * SLAB
    return pl.pallas_call(
        functools.partial(integrals_kernel, count, sent),
        in_specs=in_vmem(3 + count),
        out_specs=in_vmem(1 + len(sent)),
        out_shape=[jax.ShapeDtypeStruct((3 * SLAB, columns), BF16)]
        + [jax.ShapeDtypeStruct((2, SLAB, SLAB), BF16)] * len(sent),
        scratch_shapes=[pltpu.VMEM((3 * SLAB, columns), F32)],
        cost_estimate=pl.CostEstimate(
            flops=2 * 3 * SLAB * columns * width,
            bytes_accessed=(3 + count) * SLAB * width * 2,
            transcendentals=0,
        ),
        compiler_params=pltpu.CompilerParams(vmem_limit_bytes=8 << 20),
        name="integrals",
    )(*rows, *pieces)


def density_kernel(visit, e_occ, e_vir, early_ref, late_ref, *refs):
    swapped_refs, refs = (refs[: N_SLABS - 1], refs[N_SLABS - 1 :]) if visit else (None, refs)
    pieces, refs = refs[:N_SLABS], refs[N_SLABS:]
    before_ref = refs[0]
    out_ref, amp = refs[-2:]
    group, core = lax.axis_index("z") * XH + lax.axis_index("xh"), lax.axis_index("core")
    j = CORE * group + core
    pair = e_occ[lax.rem(j + visit, CORE * GROUPS)] + e_occ[j]
    e_a = jnp.broadcast_to(e_vir[slab_of(TURNED if visit else 0)], (SLAB, SLAB)).T
    for q in range(N_SLABS):
        direct_ref, p = (early_ref, q) if q < EARLY else (late_ref, q - EARLY)
        d = direct_ref[visit * SLAB : (visit + 1) * SLAB, p * SLAB : (p + 1) * SLAB].astype(F32)
        if visit == 0:
            s = d
        elif q == TURNED:
            s = d.T
        else:
            s = swapped_refs[q - (q > TURNED)][visit - 1].astype(F32)
        denom = pair - e_a - e_vir[slab_of(q)]
        amp[:, q * SLAB : (q + 1) * SLAB] = ((2.0 * d - s) / denom).astype(BF16)

    @pl.loop(0, pieces[0].shape[1] // STEP)
    def _(k):
        part = pl.ds(pl.multiple_of(k * STEP, STEP), STEP)
        right = jnp.concatenate([r[:, part] for r in pieces], axis=0)
        out = jnp.dot(amp[...], right, preferred_element_type=F32)
        if visit == 0:
            out = out + before_ref[:, part]
        out_ref[:, part] = out.astype(out_ref.dtype)


def density(visit, e_occ, e_vir, direct, swapped, pieces, before):
    width = pieces[0].shape[1]
    operands = [e_vir, *direct, *(swapped if visit else []), *pieces] + ([] if before is None else [before])
    return pl.pallas_call(
        functools.partial(density_kernel, visit),
        in_specs=[pl.BlockSpec(memory_space=pltpu.SMEM)] + in_vmem(len(operands)),
        out_specs=in_vmem(1)[0],
        out_shape=jax.ShapeDtypeStruct((SLAB, width), BF16 if visit else F32),
        scratch_shapes=[pltpu.VMEM((SLAB, N_SLABS * SLAB), BF16)],
        cost_estimate=pl.CostEstimate(
            flops=2 * SLAB * N_SLABS * SLAB * width,
            bytes_accessed=(1 + N_SLABS) * SLAB * width * 2,
            transcendentals=0,
        ),
        compiler_params=pltpu.CompilerParams(vmem_limit_bytes=8 << 20),
        name="density",
    )(e_occ, *operands)


def on_device(factors, occ_energy, vir_energy, density_in):
    width = factors.shape[2]
    core = lax.axis_index("core")
    home = factors.reshape(SLAB, width)
    e_vir = vir_energy.reshape(N_SLABS, 1, SLAB)
    pieces = gathered(home)
    next_2 = two_blocks_on(home, -1)
    next_1 = to_sibling(jnp.where(core == 0, next_2, pieces[TURNED]))
    rows = [home, next_1, next_2]
    sent = tuple(q for q in range(EARLY) if q != TURNED)
    early, *tiles = integrals(rows, pieces[:EARLY], sent)
    swapped = exchanged(dict(zip(sent, tiles)))
    last = [after(piece, early, *swapped.values()) for piece in pieces[EARLY:]]
    pieces = pieces[:EARLY] + last
    late, tile = integrals(rows, last, (0,))
    swapped |= exchanged({EARLY: tile})
    swapped = [swapped[q] for q in range(N_SLABS) if q != TURNED]
    given = (occ_energy, e_vir, (early, late), swapped, pieces)
    part_1 = density(1, *given, None)
    going = density(2, *given, None).astype(F32) + one_block_on(part_1, 1).astype(F32)
    back = two_blocks_on(going.astype(BF16), 1)
    total = density(0, *given, density_in.reshape(SLAB, width))
    total = total + one_block_on(part_1, 0).astype(F32) + back.astype(F32)
    return total.reshape(density_in.shape)


def solution(mesh):
    fine = Mesh(mesh.devices.reshape(Z, XH, CORE, XL, Y), AXES)
    split = P(("z", "xh", "core"), ("xl", "y"), None)
    return jax.shard_map(
        on_device,
        mesh=fine,
        in_specs=(split, P(), P(), split),
        out_specs=split,
        check_vma=False,
    )
```

```python
import functools

import jax
import jax.numpy as jnp
from jax import lax
from jax.experimental import pallas as pl
from jax.experimental.pallas import tpu as pltpu
from jax.sharding import Mesh
from jax.sharding import PartitionSpec as P

Z, XH, CORE, XL, Y = 8, 2, 2, 2, 4
GROUPS = Z * XH
AXES = ("z", "xh", "core", "xl", "y")
SLAB = 128
N_SLABS = XL * Y
PIECES = ((0, 0), (0, -1), (0, 1), (0, 2), (1, 0), (1, -1), (1, 1), (1, 2))
BACK = (0, 2, 1, 3, 4, 6, 5, 7)
INNER = 1536
STEP = 512
EARLY = 7
TURNED = 4
BF16, F32 = jnp.bfloat16, jnp.float32


def two_blocks_on(block, step):
    pairs = []
    for g in range(GROUPS):
        for c in range(CORE):
            for x in range(XL):
                to = (g + step) % GROUPS * CORE + c
                pairs.append(((g * CORE + c) * XL + x, to * XL + 1 - x))
    return lax.ppermute(block, ("z", "xh", "core", "xl"), pairs)


def one_block_on(block, core):
    return lax.ppermute(block, ("core", "xl"), [(core * XL + x, (1 - core) * XL + (x if core else 1 - x)) for x in range(XL)])


def to_sibling(block):
    return lax.ppermute(block, "core", [(0, 1), (1, 0)])


def within(block, across, step):
    pairs = []
    for c in range(CORE):
        sign = 1 - 2 * c
        for x in range(XL):
            for y in range(Y):
                to = (x ^ across) * Y + (y + sign * step) % Y
                pairs.append((c * N_SLABS + x * Y + y, c * N_SLABS + to))
    return lax.ppermute(block, ("core", "xl", "y"), pairs)


def after(block, *done):
    return lax.optimization_barrier((block, *done))[0]


def gathered(home):
    cross = within(home, 1, 0)
    down = within(home, 0, 1)
    up = within(home, 0, -1)
    far = within(down, 0, 1)
    cross_up = within(up, 1, 0)
    cross_down = within(after(cross, down, up), 0, 1)
    cross_far = within(after(cross_down, far), 0, 1)
    return [home, down, up, far, cross, cross_down, cross_up, cross_far]


def exchanged(tiles):
    return {BACK[q]: within(tile, 1 - PIECES[q][0], PIECES[q][1]) for q, tile in tiles.items()}


def slab_of(q):
    across, step = PIECES[q]
    x, y = lax.axis_index("xl"), lax.axis_index("y")
    x = 1 - x if across else x
    return x * Y + lax.rem(y + step * (1 - 2 * lax.axis_index("core")) + Y, Y)


def in_vmem(count):
    return [pl.BlockSpec(memory_space=pltpu.VMEM)] * count


def integrals_kernel(count, sent, *refs):
    rows, pieces, refs = refs[:3], refs[3 : 3 + count], refs[3 + count :]
    direct_ref, tile_refs, total = refs[0], refs[1:-1], refs[-1]
    total[...] = jnp.zeros_like(total)

    @pl.loop(0, rows[0].shape[1] // INNER)
    def _(k):
        part = pl.ds(pl.multiple_of(k * INNER, INNER), INNER)
        left = jnp.concatenate([r[:, part] for r in rows], axis=0)
        right = jnp.concatenate([r[:, part] for r in pieces], axis=0)
        total[...] += lax.dot_general(left, right, (((1,), (1,)), ((), ())), preferred_element_type=F32)

    direct_ref[...] = total[...].astype(BF16)
    for at, tile_ref in zip(sent, tile_refs):
        for v in range(2):
            tile_ref[v] = total[(v + 1) * SLAB : (v + 2) * SLAB, at * SLAB : (at + 1) * SLAB].T.astype(BF16)


def integrals(rows, pieces, sent):
    width = rows[0].shape[1]
    count = len(pieces)
    columns = count * SLAB
    return pl.pallas_call(
        functools.partial(integrals_kernel, count, sent),
        in_specs=in_vmem(3 + count),
        out_specs=in_vmem(1 + len(sent)),
        out_shape=[jax.ShapeDtypeStruct((3 * SLAB, columns), BF16)]
        + [jax.ShapeDtypeStruct((2, SLAB, SLAB), BF16)] * len(sent),
        scratch_shapes=[pltpu.VMEM((3 * SLAB, columns), F32)],
        cost_estimate=pl.CostEstimate(
            flops=2 * 3 * SLAB * columns * width,
            bytes_accessed=(3 + count) * SLAB * width * 2,
            transcendentals=0,
        ),
        compiler_params=pltpu.CompilerParams(vmem_limit_bytes=10 << 20),
        name="integrals",
    )(*rows, *pieces)


def density_kernel(visit, e_occ, e_vir, early_ref, late_ref, *refs):
    swapped_refs, refs = (refs[: N_SLABS - 1], refs[N_SLABS - 1 :]) if visit else (None, refs)
    pieces, refs = refs[:N_SLABS], refs[N_SLABS:]
    before_ref = refs[0]
    out_ref, amp = refs[-2:]
    group, core = lax.axis_index("z") * XH + lax.axis_index("xh"), lax.axis_index("core")
    j = CORE * group + core
    pair = e_occ[lax.rem(j + visit, CORE * GROUPS)] + e_occ[j]
    e_a = jnp.broadcast_to(e_vir[slab_of(TURNED if visit else 0)], (SLAB, SLAB)).T
    for q in range(N_SLABS):
        direct_ref, p = (early_ref, q) if q < EARLY else (late_ref, q - EARLY)
        d = direct_ref[visit * SLAB : (visit + 1) * SLAB, p * SLAB : (p + 1) * SLAB].astype(F32)
        if visit == 0:
            s = d
        elif q == TURNED:
            s = d.T
        else:
            s = swapped_refs[q - (q > TURNED)][visit - 1].astype(F32)
        denom = pair - e_a - e_vir[slab_of(q)]
        amp[:, q * SLAB : (q + 1) * SLAB] = ((2.0 * d - s) / denom).astype(BF16)

    @pl.loop(0, pieces[0].shape[1] // STEP)
    def _(k):
        part = pl.ds(pl.multiple_of(k * STEP, STEP), STEP)
        right = jnp.concatenate([r[:, part] for r in pieces], axis=0)
        out = jnp.dot(amp[...], right, preferred_element_type=F32)
        if visit == 0:
            out = out + before_ref[:, part]
        out_ref[:, part] = out.astype(out_ref.dtype)


def density(visit, e_occ, e_vir, direct, swapped, pieces, before):
    width = pieces[0].shape[1]
    operands = [e_vir, *direct, *(swapped if visit else []), *pieces] + ([] if before is None else [before])
    return pl.pallas_call(
        functools.partial(density_kernel, visit),
        in_specs=[pl.BlockSpec(memory_space=pltpu.SMEM)] + in_vmem(len(operands)),
        out_specs=in_vmem(1)[0],
        out_shape=jax.ShapeDtypeStruct((SLAB, width), BF16 if visit else F32),
        scratch_shapes=[pltpu.VMEM((SLAB, N_SLABS * SLAB), BF16)],
        cost_estimate=pl.CostEstimate(
            flops=2 * SLAB * N_SLABS * SLAB * width,
            bytes_accessed=(1 + N_SLABS) * SLAB * width * 2,
            transcendentals=0,
        ),
        compiler_params=pltpu.CompilerParams(vmem_limit_bytes=10 << 20),
        name="density",
    )(e_occ, *operands)


def on_device(factors, occ_energy, vir_energy, density_in):
    width = factors.shape[2]
    core = lax.axis_index("core")
    home = factors.reshape(SLAB, width)
    e_vir = vir_energy.reshape(N_SLABS, 1, SLAB)
    pieces = gathered(home)
    next_2 = two_blocks_on(home, -1)
    next_1 = to_sibling(jnp.where(core == 0, next_2, pieces[TURNED]))
    rows = [home, next_1, next_2]
    sent = tuple(q for q in range(EARLY) if q != TURNED)
    early, *tiles = integrals(rows, pieces[:EARLY], sent)
    swapped = exchanged(dict(zip(sent, tiles)))
    last = [after(piece, early, *list(swapped.values())[:4]) for piece in pieces[EARLY:]]
    pieces = pieces[:EARLY] + last
    late, tile = integrals(rows, last, (0,))
    swapped |= exchanged({EARLY: tile})
    swapped = [swapped[q] for q in range(N_SLABS) if q != TURNED]
    given = (occ_energy, e_vir, (early, late), swapped, pieces)
    part_1 = density(1, *given, None)
    going = density(2, *given, None).astype(F32) + one_block_on(part_1, 1).astype(F32)
    back = two_blocks_on(going.astype(BF16), 1)
    total = density(0, *given, density_in.reshape(SLAB, width))
    total = total + one_block_on(part_1, 0).astype(F32) + back.astype(F32)
    return total.reshape(density_in.shape)


def solution(mesh):
    fine = Mesh(mesh.devices.reshape(Z, XH, CORE, XL, Y), AXES)
    split = P(("z", "xh", "core"), ("xl", "y"), None)
    return jax.shard_map(
        on_device,
        mesh=fine,
        in_specs=(split, P(), P(), split),
        out_specs=split,
        check_vma=False,
    )
```

```python
import functools

import jax
import jax.numpy as jnp
from jax import lax
from jax.experimental import pallas as pl
from jax.experimental.pallas import tpu as pltpu
from jax.sharding import Mesh
from jax.sharding import PartitionSpec as P

Z, XH, CORE, XL, Y = 8, 2, 2, 2, 4
GROUPS = Z * XH
AXES = ("z", "xh", "core", "xl", "y")
SLAB = 128
N_SLABS = XL * Y
PIECES = ((0, 0), (0, -1), (0, 1), (0, 2), (1, 0), (1, -1), (1, 1), (1, 2))
BACK = (0, 2, 1, 3, 4, 6, 5, 7)
STEP = 1024
EARLY = 7
TURNED = 4
BF16, F32 = jnp.bfloat16, jnp.float32


def two_blocks_on(block, step):
    pairs = []
    for g in range(GROUPS):
        for c in range(CORE):
            for x in range(XL):
                to = (g + step) % GROUPS * CORE + c
                pairs.append(((g * CORE + c) * XL + x, to * XL + 1 - x))
    return lax.ppermute(block, ("z", "xh", "core", "xl"), pairs)


def one_block_on(block, core):
    return lax.ppermute(block, ("core", "xl"), [(core * XL + x, (1 - core) * XL + (x if core else 1 - x)) for x in range(XL)])


def to_sibling(block):
    return lax.ppermute(block, "core", [(0, 1), (1, 0)])


def within(block, across, step):
    pairs = []
    for c in range(CORE):
        sign = 1 - 2 * c
        for x in range(XL):
            for y in range(Y):
                to = (x ^ across) * Y + (y + sign * step) % Y
                pairs.append((c * N_SLABS + x * Y + y, c * N_SLABS + to))
    return lax.ppermute(block, ("core", "xl", "y"), pairs)


def after(block, *done):
    return lax.optimization_barrier((block, *done))[0]


def gathered(home):
    cross = within(home, 1, 0)
    down = within(home, 0, 1)
    up = within(home, 0, -1)
    far = within(down, 0, 1)
    cross_up = within(up, 1, 0)
    cross_down = within(after(cross, down, up), 0, 1)
    cross_far = within(after(cross_down, far), 0, 1)
    return [home, down, up, far, cross, cross_down, cross_up, cross_far]


def exchanged(tiles):
    return {BACK[q]: within(tile, 1 - PIECES[q][0], PIECES[q][1]) for q, tile in tiles.items()}


def slab_of(q):
    across, step = PIECES[q]
    x, y = lax.axis_index("xl"), lax.axis_index("y")
    x = 1 - x if across else x
    return x * Y + lax.rem(y + step * (1 - 2 * lax.axis_index("core")) + Y, Y)


def in_vmem(count):
    return [pl.BlockSpec(memory_space=pltpu.VMEM)] * count


def integrals_kernel(count, sent, *refs):
    rows, pieces, refs = refs[:3], refs[3 : 3 + count], refs[3 + count :]
    direct_ref, tile_refs, total = refs[0], refs[1:-1], refs[-1]
    inner = rows[0].shape[1] // (2 if count > 1 else 1)
    total[...] = jnp.zeros_like(total)

    @pl.loop(0, rows[0].shape[1] // inner)
    def _(k):
        part = pl.ds(pl.multiple_of(k * inner, inner), inner)
        left = jnp.concatenate([r[:, part] for r in rows], axis=0)
        right = jnp.concatenate([r[:, part] for r in pieces], axis=0)
        total[...] += lax.dot_general(left, right, (((1,), (1,)), ((), ())), preferred_element_type=F32)

    direct_ref[...] = total[...].astype(BF16)
    for at, tile_ref in zip(sent, tile_refs):
        for v in range(2):
            tile_ref[v] = total[(v + 1) * SLAB : (v + 2) * SLAB, at * SLAB : (at + 1) * SLAB].T.astype(BF16)


def integrals(rows, pieces, sent):
    width = rows[0].shape[1]
    count = len(pieces)
    columns = count * SLAB
    return pl.pallas_call(
        functools.partial(integrals_kernel, count, sent),
        in_specs=in_vmem(3 + count),
        out_specs=in_vmem(1 + len(sent)),
        out_shape=[jax.ShapeDtypeStruct((3 * SLAB, columns), BF16)]
        + [jax.ShapeDtypeStruct((2, SLAB, SLAB), BF16)] * len(sent),
        scratch_shapes=[pltpu.VMEM((3 * SLAB, columns), F32)],
        cost_estimate=pl.CostEstimate(
            flops=2 * 3 * SLAB * columns * width,
            bytes_accessed=(3 + count) * SLAB * width * 2,
            transcendentals=0,
        ),
        compiler_params=pltpu.CompilerParams(vmem_limit_bytes=10 << 20),
        name="integrals",
    )(*rows, *pieces)


def density_kernel(visit, e_occ, e_vir, early_ref, late_ref, *refs):
    swapped_refs, refs = (refs[: N_SLABS - 1], refs[N_SLABS - 1 :]) if visit else (None, refs)
    pieces, refs = refs[:N_SLABS], refs[N_SLABS:]
    before_ref = refs[0]
    out_ref, amp = refs[-2:]
    group, core = lax.axis_index("z") * XH + lax.axis_index("xh"), lax.axis_index("core")
    j = CORE * group + core
    pair = e_occ[lax.rem(j + visit, CORE * GROUPS)] + e_occ[j]
    e_a = jnp.broadcast_to(e_vir[slab_of(TURNED if visit else 0)], (SLAB, SLAB)).T
    for q in range(N_SLABS):
        direct_ref, p = (early_ref, q) if q < EARLY else (late_ref, q - EARLY)
        d = direct_ref[visit * SLAB : (visit + 1) * SLAB, p * SLAB : (p + 1) * SLAB].astype(F32)
        if visit == 0:
            s = d
        elif q == TURNED:
            s = d.T
        else:
            s = swapped_refs[q - (q > TURNED)][visit - 1].astype(F32)
        denom = pair - e_a - e_vir[slab_of(q)]
        amp[:, q * SLAB : (q + 1) * SLAB] = ((2.0 * d - s) / denom).astype(BF16)

    @pl.loop(0, pieces[0].shape[1] // STEP)
    def _(k):
        part = pl.ds(pl.multiple_of(k * STEP, STEP), STEP)
        right = jnp.concatenate([r[:, part] for r in pieces], axis=0)
        out = jnp.dot(amp[...], right, preferred_element_type=F32)
        if visit == 0:
            out = out + before_ref[:, part]
        out_ref[:, part] = out.astype(out_ref.dtype)


def density(visit, e_occ, e_vir, direct, swapped, pieces, before):
    width = pieces[0].shape[1]
    operands = [e_vir, *direct, *(swapped if visit else []), *pieces] + ([] if before is None else [before])
    return pl.pallas_call(
        functools.partial(density_kernel, visit),
        in_specs=[pl.BlockSpec(memory_space=pltpu.SMEM)] + in_vmem(len(operands)),
        out_specs=in_vmem(1)[0],
        out_shape=jax.ShapeDtypeStruct((SLAB, width), BF16 if visit else F32),
        scratch_shapes=[pltpu.VMEM((SLAB, N_SLABS * SLAB), BF16)],
        cost_estimate=pl.CostEstimate(
            flops=2 * SLAB * N_SLABS * SLAB * width,
            bytes_accessed=(1 + N_SLABS) * SLAB * width * 2,
            transcendentals=0,
        ),
        compiler_params=pltpu.CompilerParams(vmem_limit_bytes=10 << 20),
        name="density",
    )(e_occ, *operands)


def on_device(factors, occ_energy, vir_energy, density_in):
    width = factors.shape[2]
    core = lax.axis_index("core")
    home = factors.reshape(SLAB, width)
    e_vir = vir_energy.reshape(N_SLABS, 1, SLAB)
    pieces = gathered(home)
    next_2 = two_blocks_on(home, -1)
    next_1 = to_sibling(jnp.where(core == 0, next_2, pieces[TURNED]))
    rows = [home, next_1, next_2]
    sent = tuple(q for q in range(EARLY) if q != TURNED)
    early, *tiles = integrals(rows, pieces[:EARLY], sent)
    swapped = exchanged(dict(zip(sent, tiles)))
    last = [after(piece, early, *list(swapped.values())[:2]) for piece in pieces[EARLY:]]
    pieces = pieces[:EARLY] + last
    late, tile = integrals(rows, last, (0,))
    swapped |= exchanged({EARLY: tile})
    swapped = [swapped[q] for q in range(N_SLABS) if q != TURNED]
    given = (occ_energy, e_vir, (early, late), swapped, pieces)
    part_1 = density(1, *given, None)
    going = density(2, *given, None).astype(F32) + one_block_on(part_1, 1).astype(F32)
    going = going.astype(BF16)
    back = two_blocks_on(going, 1)
    total = density(0, *given, density_in.reshape(SLAB, width))
    beside = one_block_on(after(part_1, going), 0)
    total = lax.optimization_barrier(total + back.astype(F32)) + beside.astype(F32)
    return total.reshape(density_in.shape)


def solution(mesh):
    fine = Mesh(mesh.devices.reshape(Z, XH, CORE, XL, Y), AXES)
    split = P(("z", "xh", "core"), ("xl", "y"), None)
    return jax.shard_map(
        on_device,
        mesh=fine,
        in_specs=(split, P(), P(), split),
        out_specs=split,
        check_vma=False,
    )
```

```python
import functools

import jax
import jax.numpy as jnp
from jax import lax
from jax.experimental import pallas as pl
from jax.experimental.pallas import tpu as pltpu
from jax.sharding import Mesh
from jax.sharding import PartitionSpec as P

Z, XH, CORE, XL, Y = 8, 2, 2, 2, 4
GROUPS = Z * XH
AXES = ("z", "xh", "core", "xl", "y")
SLAB = 128
N_SLABS = XL * Y
PIECES = ((0, 0), (0, -1), (0, 1), (0, 2), (1, 0), (1, -1), (1, 1), (1, 2))
BACK = (0, 2, 1, 3, 4, 6, 5, 7)
STEP = 1536
EARLY = 7
TURNED = 4
BF16, F32 = jnp.bfloat16, jnp.float32


def two_blocks_on(block, step):
    pairs = []
    for g in range(GROUPS):
        for c in range(CORE):
            for x in range(XL):
                to = (g + step) % GROUPS * CORE + c
                pairs.append(((g * CORE + c) * XL + x, to * XL + 1 - x))
    return lax.ppermute(block, ("z", "xh", "core", "xl"), pairs)


def one_block_on(block, core):
    return lax.ppermute(block, ("core", "xl"), [(core * XL + x, (1 - core) * XL + (x if core else 1 - x)) for x in range(XL)])


def to_sibling(block):
    return lax.ppermute(block, "core", [(0, 1), (1, 0)])


def within(block, across, step):
    pairs = []
    for c in range(CORE):
        sign = 1 - 2 * c
        for x in range(XL):
            for y in range(Y):
                to = (x ^ across) * Y + (y + sign * step) % Y
                pairs.append((c * N_SLABS + x * Y + y, c * N_SLABS + to))
    return lax.ppermute(block, ("core", "xl", "y"), pairs)


def after(block, *done):
    return lax.optimization_barrier((block, *done))[0]


def gathered(home):
    cross = within(home, 1, 0)
    down = within(home, 0, 1)
    up = within(home, 0, -1)
    far = within(down, 0, 1)
    cross_up = within(up, 1, 0)
    cross_down = within(after(cross, down, up), 0, 1)
    cross_far = within(after(cross_down, far), 0, 1)
    return [home, down, up, far, cross, cross_down, cross_up, cross_far]


def exchanged(tiles):
    return {BACK[q]: within(tile, 1 - PIECES[q][0], PIECES[q][1]) for q, tile in tiles.items()}


def slab_of(q):
    across, step = PIECES[q]
    x, y = lax.axis_index("xl"), lax.axis_index("y")
    x = 1 - x if across else x
    return x * Y + lax.rem(y + step * (1 - 2 * lax.axis_index("core")) + Y, Y)


def in_vmem(count):
    return [pl.BlockSpec(memory_space=pltpu.VMEM)] * count


def integrals_kernel(count, sent, *refs):
    rows, pieces, refs = refs[:3], refs[3 : 3 + count], refs[3 + count :]
    direct_ref, tile_refs, total = refs[0], refs[1:-1], refs[-1]
    inner = rows[0].shape[1] // (2 if count > 1 else 1)
    total[...] = jnp.zeros_like(total)

    @pl.loop(0, rows[0].shape[1] // inner)
    def _(k):
        part = pl.ds(pl.multiple_of(k * inner, inner), inner)
        left = jnp.concatenate([r[:, part] for r in rows], axis=0)
        right = jnp.concatenate([r[:, part] for r in pieces], axis=0)
        total[...] += lax.dot_general(left, right, (((1,), (1,)), ((), ())), preferred_element_type=F32)

    direct_ref[...] = total[...].astype(BF16)
    for at, tile_ref in zip(sent, tile_refs):
        for v in range(2):
            tile_ref[v] = total[(v + 1) * SLAB : (v + 2) * SLAB, at * SLAB : (at + 1) * SLAB].T.astype(BF16)


def integrals(rows, pieces, sent):
    width = rows[0].shape[1]
    count = len(pieces)
    columns = count * SLAB
    return pl.pallas_call(
        functools.partial(integrals_kernel, count, sent),
        in_specs=in_vmem(3 + count),
        out_specs=in_vmem(1 + len(sent)),
        out_shape=[jax.ShapeDtypeStruct((3 * SLAB, columns), BF16)]
        + [jax.ShapeDtypeStruct((2, SLAB, SLAB), BF16)] * len(sent),
        scratch_shapes=[pltpu.VMEM((3 * SLAB, columns), F32)],
        cost_estimate=pl.CostEstimate(
            flops=2 * 3 * SLAB * columns * width,
            bytes_accessed=(3 + count) * SLAB * width * 2,
            transcendentals=0,
        ),
        compiler_params=pltpu.CompilerParams(vmem_limit_bytes=10 << 20),
        name="integrals",
    )(*rows, *pieces)


def density_kernel(visit, e_occ, e_vir, early_ref, late_ref, *refs):
    swapped_refs, refs = (refs[: N_SLABS - 1], refs[N_SLABS - 1 :]) if visit else (None, refs)
    pieces, refs = refs[:N_SLABS], refs[N_SLABS:]
    before_ref = refs[0]
    out_ref, amp = refs[-2:]
    group, core = lax.axis_index("z") * XH + lax.axis_index("xh"), lax.axis_index("core")
    j = CORE * group + core
    pair = e_occ[lax.rem(j + visit, CORE * GROUPS)] + e_occ[j]
    e_a = jnp.broadcast_to(e_vir[slab_of(TURNED if visit else 0)], (SLAB, SLAB)).T
    for q in range(N_SLABS):
        direct_ref, p = (early_ref, q) if q < EARLY else (late_ref, q - EARLY)
        d = direct_ref[visit * SLAB : (visit + 1) * SLAB, p * SLAB : (p + 1) * SLAB].astype(F32)
        if visit == 0:
            s = d
        elif q == TURNED:
            s = d.T
        else:
            s = swapped_refs[q - (q > TURNED)][visit - 1].astype(F32)
        denom = pair - e_a - e_vir[slab_of(q)]
        amp[:, q * SLAB : (q + 1) * SLAB] = ((2.0 * d - s) / denom).astype(BF16)

    @pl.loop(0, pieces[0].shape[1] // STEP)
    def _(k):
        part = pl.ds(pl.multiple_of(k * STEP, STEP), STEP)
        right = jnp.concatenate([r[:, part] for r in pieces], axis=0)
        out = jnp.dot(amp[...], right, preferred_element_type=F32)
        if visit == 0:
            out = out + before_ref[:, part]
        out_ref[:, part] = out.astype(out_ref.dtype)


def density(visit, e_occ, e_vir, direct, swapped, pieces, before):
    width = pieces[0].shape[1]
    operands = [e_vir, *direct, *(swapped if visit else []), *pieces] + ([] if before is None else [before])
    return pl.pallas_call(
        functools.partial(density_kernel, visit),
        in_specs=[pl.BlockSpec(memory_space=pltpu.SMEM)] + in_vmem(len(operands)),
        out_specs=in_vmem(1)[0],
        out_shape=jax.ShapeDtypeStruct((SLAB, width), BF16 if visit else F32),
        scratch_shapes=[pltpu.VMEM((SLAB, N_SLABS * SLAB), BF16)],
        cost_estimate=pl.CostEstimate(
            flops=2 * SLAB * N_SLABS * SLAB * width,
            bytes_accessed=(1 + N_SLABS) * SLAB * width * 2,
            transcendentals=0,
        ),
        compiler_params=pltpu.CompilerParams(vmem_limit_bytes=10 << 20),
        name="density",
    )(e_occ, *operands)


def on_device(factors, occ_energy, vir_energy, density_in):
    width = factors.shape[2]
    core = lax.axis_index("core")
    home = factors.reshape(SLAB, width)
    e_vir = vir_energy.reshape(N_SLABS, 1, SLAB)
    pieces = gathered(home)
    next_2 = two_blocks_on(home, -1)
    next_1 = to_sibling(jnp.where(core == 0, next_2, pieces[TURNED]))
    rows = [home, next_1, next_2]
    sent = (3, 0, 5, 6, 1, 2)
    early, *tiles = integrals(rows, pieces[:EARLY], sent)
    swapped = exchanged(dict(zip(sent, tiles)))
    last = [after(piece, early, *list(swapped.values())[:2]) for piece in pieces[EARLY:]]
    pieces = pieces[:EARLY] + last
    late, tile = integrals(rows, last, (0,))
    swapped |= exchanged({EARLY: tile})
    swapped = [swapped[q] for q in range(N_SLABS) if q != TURNED]
    given = (occ_energy, e_vir, (early, late), swapped, pieces)
    part_1 = density(1, *given, None)
    going = density(2, *given, None).astype(F32) + one_block_on(part_1, 1).astype(F32)
    going = going.astype(BF16)
    back = two_blocks_on(going, 1)
    total = density(0, *given, density_in.reshape(SLAB, width))
    beside = one_block_on(after(part_1, going), 0)
    total = lax.optimization_barrier(total + back.astype(F32)) + beside.astype(F32)
    return total.reshape(density_in.shape)


def solution(mesh):
    fine = Mesh(mesh.devices.reshape(Z, XH, CORE, XL, Y), AXES)
    split = P(("z", "xh", "core"), ("xl", "y"), None)
    return jax.shard_map(
        on_device,
        mesh=fine,
        in_specs=(split, P(), P(), split),
        out_specs=split,
        check_vma=False,
    )
```

```python
import functools

import jax
import jax.numpy as jnp
from jax import lax
from jax.experimental import pallas as pl
from jax.experimental.pallas import tpu as pltpu
from jax.sharding import Mesh
from jax.sharding import PartitionSpec as P

Z, XH, CORE, XL, Y = 8, 2, 2, 2, 4
GROUPS = Z * XH
AXES = ("z", "xh", "core", "xl", "y")
SLAB = 128
N_SLABS = XL * Y
PIECES = ((0, 0), (0, -1), (0, 1), (0, 2), (1, 0), (1, -1), (1, 1), (1, 2))
BACK = (0, 2, 1, 3, 4, 6, 5, 7)
STEP = 1536
EARLY = 7
TURNED = 4
BF16, F32 = jnp.bfloat16, jnp.float32


def two_blocks_on(block, step):
    pairs = []
    for g in range(GROUPS):
        for c in range(CORE):
            for x in range(XL):
                to = (g + step) % GROUPS * CORE + c
                pairs.append(((g * CORE + c) * XL + x, to * XL + 1 - x))
    return lax.ppermute(block, ("z", "xh", "core", "xl"), pairs)


def one_block_on(block, core):
    return lax.ppermute(block, ("core", "xl"), [(core * XL + x, (1 - core) * XL + (x if core else 1 - x)) for x in range(XL)])


def to_sibling(block):
    return lax.ppermute(block, "core", [(0, 1), (1, 0)])


def within(block, across, step):
    pairs = []
    for c in range(CORE):
        sign = 1 - 2 * c
        for x in range(XL):
            for y in range(Y):
                to = (x ^ across) * Y + (y + sign * step) % Y
                pairs.append((c * N_SLABS + x * Y + y, c * N_SLABS + to))
    return lax.ppermute(block, ("core", "xl", "y"), pairs)


def after(block, *done):
    return lax.optimization_barrier((block, *done))[0]


def gathered(home):
    cross = within(home, 1, 0)
    down = within(home, 0, 1)
    up = within(home, 0, -1)
    far = within(down, 0, 1)
    cross_up = within(up, 1, 0)
    cross_down = within(after(cross, down, up), 0, 1)
    cross_far = within(after(cross_down, far), 0, 1)
    return [home, down, up, far, cross, cross_down, cross_up, cross_far]


def exchanged(tiles):
    return {BACK[q]: within(tile, 1 - PIECES[q][0], PIECES[q][1]) for q, tile in tiles.items()}


def slab_of(q):
    across, step = PIECES[q]
    x, y = lax.axis_index("xl"), lax.axis_index("y")
    x = 1 - x if across else x
    return x * Y + lax.rem(y + step * (1 - 2 * lax.axis_index("core")) + Y, Y)


def in_vmem(count):
    return [pl.BlockSpec(memory_space=pltpu.VMEM)] * count


def integrals_kernel(count, sent, *refs):
    rows, pieces, refs = refs[:3], refs[3 : 3 + count], refs[3 + count :]
    direct_ref, tile_refs, total = refs[0], refs[1:-1], refs[-1]
    inner = rows[0].shape[1] // (2 if count > 1 else 1)
    total[...] = jnp.zeros_like(total)

    @pl.loop(0, rows[0].shape[1] // inner)
    def _(k):
        part = pl.ds(pl.multiple_of(k * inner, inner), inner)
        left = jnp.concatenate([r[:, part] for r in rows], axis=0)
        right = jnp.concatenate([r[:, part] for r in pieces], axis=0)
        total[...] += lax.dot_general(left, right, (((1,), (1,)), ((), ())), preferred_element_type=F32)

    direct_ref[...] = total[...].astype(BF16)
    for at, tile_ref in zip(sent, tile_refs):
        for v in range(2):
            tile_ref[v] = total[(v + 1) * SLAB : (v + 2) * SLAB, at * SLAB : (at + 1) * SLAB].T.astype(BF16)


def integrals(rows, pieces, sent):
    width = rows[0].shape[1]
    count = len(pieces)
    columns = count * SLAB
    return pl.pallas_call(
        functools.partial(integrals_kernel, count, sent),
        in_specs=in_vmem(3 + count),
        out_specs=in_vmem(1 + len(sent)),
        out_shape=[jax.ShapeDtypeStruct((3 * SLAB, columns), BF16)]
        + [jax.ShapeDtypeStruct((2, SLAB, SLAB), BF16)] * len(sent),
        scratch_shapes=[pltpu.VMEM((3 * SLAB, columns), F32)],
        cost_estimate=pl.CostEstimate(
            flops=2 * 3 * SLAB * columns * width,
            bytes_accessed=(3 + count) * SLAB * width * 2,
            transcendentals=0,
        ),
        compiler_params=pltpu.CompilerParams(vmem_limit_bytes=10 << 20),
        name="integrals",
    )(*rows, *pieces)


def density_kernel(visit, e_occ, e_vir, early_ref, late_ref, *refs):
    swapped_refs, refs = (refs[: N_SLABS - 1], refs[N_SLABS - 1 :]) if visit else (None, refs)
    pieces, refs = refs[:N_SLABS], refs[N_SLABS:]
    before_ref = refs[0]
    out_ref, amp = refs[-2:]
    group, core = lax.axis_index("z") * XH + lax.axis_index("xh"), lax.axis_index("core")
    j = CORE * group + core
    pair = e_occ[lax.rem(j + visit, CORE * GROUPS)] + e_occ[j]
    e_a = jnp.broadcast_to(e_vir[slab_of(TURNED if visit else 0)], (SLAB, SLAB)).T
    for q in range(N_SLABS):
        direct_ref, p = (early_ref, q) if q < EARLY else (late_ref, q - EARLY)
        d = direct_ref[visit * SLAB : (visit + 1) * SLAB, p * SLAB : (p + 1) * SLAB].astype(F32)
        if visit == 0:
            s = d
        elif q == TURNED:
            s = d.T
        else:
            s = swapped_refs[q - (q > TURNED)][visit - 1].astype(F32)
        denom = pair - e_a - e_vir[slab_of(q)]
        amp[:, q * SLAB : (q + 1) * SLAB] = ((2.0 * d - s) / denom).astype(BF16)

    @pl.loop(0, pieces[0].shape[1] // STEP)
    def _(k):
        part = pl.ds(pl.multiple_of(k * STEP, STEP), STEP)
        right = jnp.concatenate([r[:, part] for r in pieces], axis=0)
        out = jnp.dot(amp[...], right, preferred_element_type=F32)
        if visit == 0:
            out = out + before_ref[:, part]
        out_ref[:, part] = out.astype(out_ref.dtype)


def density(visit, e_occ, e_vir, direct, swapped, pieces, before):
    width = pieces[0].shape[1]
    operands = [e_vir, *direct, *(swapped if visit else []), *pieces] + ([] if before is None else [before])
    return pl.pallas_call(
        functools.partial(density_kernel, visit),
        in_specs=[pl.BlockSpec(memory_space=pltpu.SMEM)] + in_vmem(len(operands)),
        out_specs=in_vmem(1)[0],
        out_shape=jax.ShapeDtypeStruct((SLAB, width), BF16 if visit else F32),
        scratch_shapes=[pltpu.VMEM((SLAB, N_SLABS * SLAB), BF16)],
        cost_estimate=pl.CostEstimate(
            flops=2 * SLAB * N_SLABS * SLAB * width,
            bytes_accessed=(1 + N_SLABS) * SLAB * width * 2,
            transcendentals=0,
        ),
        compiler_params=pltpu.CompilerParams(vmem_limit_bytes=10 << 20),
        name="density",
    )(e_occ, *operands)


def on_device(factors, occ_energy, vir_energy, density_in):
    width = factors.shape[2]
    core = lax.axis_index("core")
    home = factors.reshape(SLAB, width)
    e_vir = vir_energy.reshape(N_SLABS, 1, SLAB)
    pieces = gathered(home)
    next_2 = two_blocks_on(home, -1)
    next_1 = to_sibling(jnp.where(core == 0, next_2, pieces[TURNED]))
    rows = [home, next_1, next_2]
    sent = (3, 0, 5, 6, 1, 2)
    early, *tiles = integrals(rows, pieces[:EARLY], sent)
    swapped = exchanged(dict(zip(sent, tiles)))
    last = [after(piece, early, *list(swapped.values())[:3]) for piece in pieces[EARLY:]]
    pieces = pieces[:EARLY] + last
    late, tile = integrals(rows, last, (0,))
    swapped |= exchanged({EARLY: tile})
    swapped = [swapped[q] for q in range(N_SLABS) if q != TURNED]
    given = (occ_energy, e_vir, (early, late), swapped, pieces)
    part_1 = density(1, *given, None)
    going = density(2, *given, None).astype(F32) + one_block_on(part_1, 1).astype(F32)
    going = going.astype(BF16)
    back = two_blocks_on(going, 1)
    total = density(0, *given, density_in.reshape(SLAB, width))
    beside = one_block_on(after(part_1, going), 0)
    total = lax.optimization_barrier(total + back.astype(F32)) + beside.astype(F32)
    return total.reshape(density_in.shape)


def solution(mesh):
    fine = Mesh(mesh.devices.reshape(Z, XH, CORE, XL, Y), AXES)
    split = P(("z", "xh", "core"), ("xl", "y"), None)
    return jax.shard_map(
        on_device,
        mesh=fine,
        in_specs=(split, P(), P(), split),
        out_specs=split,
        check_vma=False,
    )
```
